32 devices in a mesh: expert: 16 (over z, y, x), dp: 2 (over core).
Axes of the slice: x: 2, y: 2, z: 4, core: 2. Of those that a mesh axis runs over, the one named last changes fastest.
Arguments:
- tokens: bfloat16 [4096, 2048], P(('expert', 'dp')), may hold values from -6 to 6
- routes: int32 [4096, 8], P(('expert', 'dp')), may hold values from 0 to 15, all different within a row; in each aligned block of 128 rows (0 to 127, 128 to 255, ...) at most 72 rows name the same one
- gates: float32 [4096, 8], P(('expert', 'dp')), may hold values from 0.05 to 1
- cotangent: bfloat16 [4096, 2048], P(('expert', 'dp')), may hold values from -6 to 6
- owner_before: int32 [16], replicated, may hold values from 0 to 15, each once
- owner_after: int32 [16], replicated, may hold values from 0 to 15, each once
- weights: bfloat16 [2, 16, 2048, 768], P(None, 'expert', 'dp'), may hold values from -6 to 6
- m_codes: bfloat16 [2, 16, 2048, 768], P(None, 'expert', 'dp'), may hold values from -7 to 7, as said below
- v_codes: bfloat16 [2, 16, 2048, 768], P(None, 'expert', 'dp'), may hold values from 1 to 7, as said below
- m_scales: bfloat16 [2, 16, 2048], P(None, 'expert', 'dp'), may hold values from 0.049804688 to 0.5
- v_scales: bfloat16 [2, 16, 2048], P(None, 'expert', 'dp'), may hold values from 0.019897461 to 0.19921875
- noise: bfloat16 [2, 16, 2048, 768], P(None, 'expert', 'dp'), may hold values from 0 to 1
Outputs:
- new_weights: bfloat16 [2, 16, 2048, 768], P(None, 'expert', 'dp')
- new_m_codes: bfloat16 [2, 16, 2048, 768], P(None, 'expert', 'dp')
- new_v_codes: bfloat16 [2, 16, 2048, 768], P(None, 'expert', 'dp')
- new_m_scales: bfloat16 [2, 16, 2048], P(None, 'expert', 'dp')
- new_v_scales: bfloat16 [2, 16, 2048], P(None, 'expert', 'dp')
The draws below stay inside these ranges and needn't reach their ends.
Inputs may be any that keep to these rules, and one draw needn't show every extreme that they name: `routes`: in the rows of one device no expert is chosen by more than 72 tokens; each token chooses 8 different experts. `owner_before`: A permutation of the slots. `owner_after`: A permutation of the slots. `m_codes`: whole numbers. `v_codes`: whole numbers.
All inputs are finite; a program needn't handle non-finite values. Where the reference program divides by a largest or mean magnitude, that divisor is 1e-20 or more.
Results may differ from the reference program's by a relative error of at most 0.022.
Values may be sent and summed in bfloat16 or wider, within the bound.
A program may use at most 128 MiB of HBM per device.

```python
import math
import jax
import jax.numpy as jnp
import numpy as np
from jax import lax

D = 2048
FF = 768
TOP = 8
LEVELS = 7
TOK_DEV = 128
CAP = 72
EXPERTS = 16
TOKENS = 4096
N_EXPERT = 16
N_DP = 2


def draw_m_codes(key, part):
    whole = jax.random.randint(jax.random.fold_in(key, 11), (2, EXPERTS, D, FF), -LEVELS, LEVELS + 1, dtype=jnp.int32)
    return whole.astype(jnp.float32).astype(jnp.bfloat16)


def draw_v_codes(key, part):
    whole = jax.random.randint(jax.random.fold_in(key, 23), (2, EXPERTS, D, FF), 1, LEVELS + 1, dtype=jnp.int32)
    return whole.astype(jnp.float32).astype(jnp.bfloat16)


def block_scale(stream_key, dims, pieces, smallest, largest):
    factor_of, own = 1.0, jax.random.fold_in(stream_key, 6)
    for axis_at, parts in pieces:
        steps = jnp.exp(jax.random.uniform(jax.random.fold_in(own, axis_at), (parts,), jnp.float32, smallest / len(pieces), largest / len(pieces)))
        factor_of = factor_of * jnp.repeat(steps, dims[axis_at] // parts).reshape([-1 if axis == axis_at else 1 for axis in range(len(dims))])
    return factor_of


def deal_out(key, own, number, rows, amount, top, reach, lean):
    sequence = jax.random.permutation(key, amount)
    packed, common = shares(amount, rows * top, reach, lean, True), shares(amount, rows * top, reach, lean, False)
    places = jnp.arange(amount)

    def named(lengths, offset_by):
        used = int((lengths > 0).sum())
        fixed = max(1, used // 4)
        moved = fixed + (places - fixed + offset_by * (used - fixed)) % max(1, amount - fixed)
        return jnp.zeros((amount,), jnp.int32).at[sequence[jnp.where(places < fixed, places, moved)]].set(jnp.asarray(lengths, jnp.int32))

    lengths = jnp.where(number % 4 == 0, named(packed, number // 4), named(common, number - number // 4 - 1))
    mixed = jax.random.permutation(jax.random.fold_in(own, 3), amount)
    donor, sink = mixed[0:amount // 2 * 2:2], mixed[1:amount // 2 * 2:2]
    margin = jnp.minimum(lengths[donor] - 1, reach - lengths[sink]) // 2
    margin = jnp.where((donor == sequence[0]) | (sink == sequence[0]) | (lengths[sink] == 0), 0, jnp.maximum(margin, 0))
    moved = jax.random.randint(jax.random.fold_in(own, 4), (amount // 2,), 0, 1 << 20) % (margin + 1)
    lengths = lengths.at[donor].add(-moved).at[sink].add(moved)
    members = jnp.searchsorted(jnp.cumsum(lengths), jnp.arange(rows * top), side="right").astype(jnp.int32)
    table = members.reshape(top, rows).T
    table = table[jax.random.permutation(jax.random.fold_in(own, 1), rows)]
    offset_by = jax.random.randint(jax.random.fold_in(own, 2), (rows, 1), 0, top)
    return jnp.take_along_axis(table, (jnp.arange(top)[None, :] + offset_by) % top, axis=1)


def shares(count, total, reach, skew, full):
    portions = [(1 << 20) // math.isqrt(standing ** skew) + 1 for standing in range(1, count + 1)]
    largest = reach if full else min(reach, max(-(-total // count), total * portions[0] // sum(portions)))
    least = 1 if total - largest >= count - 1 else 0
    counts, surplus = [largest] + [least] * (count - 1), total - largest - least * (count - 1)
    while surplus > 0:
        candidates = [i for i in range(1, count) if counts[i] < largest] or [i for i in range(1, count) if counts[i] < reach]
        mass, left = sum([portions[i] for i in candidates]), surplus
        for i in candidates:
            more = min(reach - counts[i], max(1, left * portions[i] // mass), surplus)
            counts[i] = counts[i] + more
            surplus = surplus - more
    return np.array(counts)


def normal_values(stream_key, dims, scale, most, pieces=(), kind=jnp.bfloat16):
    array = scale * jax.random.normal(stream_key, dims, jnp.float32)
    if pieces:
        array = array * block_scale(stream_key, dims, pieces, -0.22, 0.18)
    return jnp.clip(array, -most, most).astype(kind)


def setup_inputs(seed: int = 0) -> dict:
    key_of = jax.random.split(jax.random.key(seed), 13)
    tokens = normal_values(key_of[0], (TOKENS, D), 1.0, 6.0, ((0, 32),))
    routes_keys = jax.random.split(jax.random.fold_in(key_of[1], 1), TOKENS // TOK_DEV)
    routes_turns = jax.random.permutation(jax.random.fold_in(key_of[1], 3), TOKENS // TOK_DEV)
    routes = jax.vmap(lambda own, number: deal_out(jax.random.fold_in(key_of[1], 2), own, number, TOK_DEV, EXPERTS, TOP, CAP, 0))(routes_keys, routes_turns).reshape((TOKENS, TOP))
    gates = jnp.clip(jnp.exp(math.log(1.0) - 2.9957323 * jax.random.uniform(key_of[2], (TOKENS, TOP), jnp.float32) ** block_scale(key_of[2], (TOKENS, TOP), ((0, 32),), -0.2, 0.2)), 0.05, 1.0)
    cotangent = normal_values(key_of[3], (TOKENS, D), 1.0, 6.0, ((0, 32),))
    owner_before = jax.random.permutation(key_of[4], EXPERTS).astype(jnp.int32)
    owner_after = jax.random.permutation(key_of[5], EXPERTS).astype(jnp.int32)
    weights = normal_values(key_of[6], (2, EXPERTS, D, FF), 1.0, 6.0, ((1, 16), (2, 2)))
    m_codes = draw_m_codes(jax.random.fold_in(key_of[12], 71), 0)
    v_codes = draw_v_codes(jax.random.fold_in(key_of[12], 71), 0)
    m_scales = jnp.clip(jnp.exp(math.log(0.5) - 2.306499 * jax.random.uniform(key_of[9], (2, EXPERTS, D), jnp.float32) ** block_scale(key_of[9], (2, EXPERTS, D), ((1, 16), (2, 2)), -0.2, 0.2)), 0.049804688, 0.5).astype(jnp.bfloat16)
    v_scales = jnp.clip(jnp.exp(math.log(0.19921875) - 2.3038113 * jax.random.uniform(key_of[10], (2, EXPERTS, D), jnp.float32) ** block_scale(key_of[10], (2, EXPERTS, D), ((1, 16), (2, 2)), -0.2, 0.2)), 0.019897461, 0.19921875).astype(jnp.bfloat16)
    noise = jnp.clip(1.0 * jax.random.uniform(key_of[11], (2, EXPERTS, D, FF), jnp.float32) ** block_scale(key_of[11], (2, EXPERTS, D, FF), ((1, 16), (2, 2)), -0.2, 0.2), 0.0, 1.0).astype(jnp.bfloat16)
    return dict(tokens=tokens, routes=routes, gates=gates, cotangent=cotangent, owner_before=owner_before, owner_after=owner_after, weights=weights, m_codes=m_codes, v_codes=v_codes, m_scales=m_scales, v_scales=v_scales, noise=noise)


learn_rate = 0.1
beta_one = 0.9
beta_two = 0.95
adam_step = 20.0
adam_epsilon = 1e-08
scale_epsilon = 1e-06

def transposed_dot(left, right):
    return lax.dot_general(left, right, (((0,), (0,)), ((), ())), preferred_element_type=jnp.float32)

def slot_table(routes):
    device_count = N_EXPERT * N_DP
    entries = routes.reshape(device_count, TOK_DEV * TOP)
    expert_ids = jnp.arange(EXPERTS, dtype=jnp.int32)
    onehot = (entries[:, :, None] == expert_ids[None, None, :]).astype(jnp.int32)
    ranks = lax.optimization_barrier(jnp.sum((jnp.cumsum(onehot, axis=1) - 1) * onehot, axis=2)).astype(jnp.int32)
    sources = jnp.broadcast_to(jnp.arange(device_count, dtype=jnp.int32)[:, None], entries.shape)
    locals_ids = jnp.broadcast_to(jnp.arange(TOK_DEV * TOP, dtype=jnp.int32)[None, :], entries.shape)
    flat_ids = (sources * (TOK_DEV * TOP) + locals_ids).astype(jnp.int32)
    table = jnp.full((EXPERTS, device_count, CAP), -1, jnp.int32)
    return table.at[entries, sources, ranks].set(flat_ids)

def reference(tokens, routes, gates, cotangent, owner_before, owner_after, weights, m_codes, v_codes, m_scales, v_scales, noise):
    table = slot_table(routes)
    flat_gates = gates.reshape(-1)
    slot_ids = jnp.arange(EXPERTS, dtype=jnp.int32)
    holder = jnp.zeros((EXPERTS,), jnp.int32).at[owner_after].set(slot_ids)
    scale_model = D ** (-0.5)
    scale_hidden = FF ** (-0.5)

    def replica_grads(expert, replica, w_up, w_down):
        sources = (jnp.arange(N_EXPERT, dtype=jnp.int32) * N_DP + replica).astype(jnp.int32)
        entry = table[expert][sources].reshape(-1)
        live = entry >= 0
        safe = jnp.where(live, entry, 0).astype(jnp.int32)
        token_rows = (safe // TOP).astype(jnp.int32)
        token_block = jnp.where(live[:, None], tokens[token_rows], jnp.zeros((), tokens.dtype))
        gate_rows = jnp.where(live, flat_gates[safe], jnp.zeros((), flat_gates.dtype))
        gated_block = (gate_rows[:, None] * cotangent[token_rows].astype(jnp.float32)).astype(jnp.bfloat16)
        pre = jnp.dot(token_block, w_up, preferred_element_type=jnp.float32) * scale_model
        hidden = jax.nn.silu(pre).astype(jnp.bfloat16)
        back = jnp.dot(gated_block, w_down, preferred_element_type=jnp.float32) * scale_hidden
        sigmoid_pre = jax.nn.sigmoid(pre)
        pre_grad = (back * sigmoid_pre * (1.0 + pre * (1.0 - sigmoid_pre))).astype(jnp.bfloat16)
        up_part = transposed_dot(token_block, pre_grad) * scale_model
        down_part = transposed_dot(gated_block, hidden) * scale_hidden
        rounded = lax.optimization_barrier(jnp.stack([up_part, down_part]).astype(jnp.bfloat16))
        return rounded.astype(jnp.float32)

    def update_slot(slot):
        expert = holder[slot]
        old_slot = owner_before[expert]
        w_old = weights[:, old_slot]

        def add_replica(replica, total):
            return total + replica_grads(expert, replica, w_old[0], w_old[1])
        grads = lax.fori_loop(0, N_DP, add_replica, jnp.zeros((2, D, FF), jnp.float32))
        m_old = m_codes[:, old_slot].astype(jnp.float32) * m_scales[:, old_slot].astype(jnp.float32)[:, :, None] / LEVELS
        v_old = v_codes[:, old_slot].astype(jnp.float32) * v_scales[:, old_slot].astype(jnp.float32)[:, :, None] / LEVELS
        m_new = beta_one * m_old + (1.0 - beta_one) * grads
        v_new = beta_two * v_old + (1.0 - beta_two) * grads * grads
        direction = m_new / (1.0 - beta_one ** adam_step) / (jnp.sqrt(v_new / (1.0 - beta_two ** adam_step)) + adam_epsilon)
        new_w = (w_old.astype(jnp.float32) - learn_rate * direction).astype(jnp.bfloat16)
        new_ms = lax.optimization_barrier((lax.optimization_barrier(jnp.max(jnp.abs(m_new), axis=2)) + scale_epsilon).astype(jnp.bfloat16))
        new_vs = lax.optimization_barrier((lax.optimization_barrier(jnp.max(v_new, axis=2)) + scale_epsilon).astype(jnp.bfloat16))
        dither = noise[:, slot].astype(jnp.float32)
        m_value = LEVELS * m_new / new_ms.astype(jnp.float32)[:, :, None] + (dither - 0.5)
        v_value = LEVELS * v_new / new_vs.astype(jnp.float32)[:, :, None] + dither
        new_mc = jnp.clip(m_value, -1.0 * LEVELS, 1.0 * LEVELS).astype(jnp.bfloat16)
        new_vc = jnp.clip(v_value, 0.0, 1.0 * LEVELS).astype(jnp.bfloat16)
        return (new_w, new_mc, new_vc, new_ms, new_vs)
    results = lax.map(update_slot, slot_ids)
    return (jnp.moveaxis(results[0], 0, 1), jnp.moveaxis(results[1], 0, 1), jnp.moveaxis(results[2], 0, 1), jnp.moveaxis(results[3], 0, 1), jnp.moveaxis(results[4], 0, 1))
```

```python
import functools

import jax
import jax.numpy as jnp
from jax import lax
from jax.experimental import pallas as pl
from jax.experimental.pallas import tpu as pltpu
from jax.sharding import PartitionSpec as P

LEVELS = 7


learn_rate = 0.1
beta_one = 0.9
beta_two = 0.95
adam_step = 20.0
adam_epsilon = 1e-08
scale_epsilon = 1e-06


def transposed_dot(left, right):
    return lax.dot_general(
        left, right, (((0,), (0,)), ((), ())), preferred_element_type=jnp.float32
    )


def adam_kernel(grad, weight, m_code, v_code, m_scale, v_scale, noise, new_w, new_m, new_v, new_ms, new_vs):
    grads = grad[...].astype(jnp.float32)
    m_old = m_code[...].astype(jnp.float32) * (m_scale[...].astype(jnp.float32) / LEVELS)
    v_old = v_code[...].astype(jnp.float32) * (v_scale[...].astype(jnp.float32) / LEVELS)
    m_new = beta_one * m_old + (1.0 - beta_one) * grads
    v_new = beta_two * v_old + (1.0 - beta_two) * grads * grads
    direction = (
        m_new
        * (1.0 / (1.0 - beta_one**adam_step))
        / (jnp.sqrt(v_new * (1.0 / (1.0 - beta_two**adam_step))) + adam_epsilon)
    )
    new_w[...] = (weight[...].astype(jnp.float32) - learn_rate * direction).astype(jnp.bfloat16)
    m_top = (jnp.max(jnp.abs(m_new), axis=1, keepdims=True) + scale_epsilon).astype(jnp.bfloat16)
    v_top = (jnp.max(v_new, axis=1, keepdims=True) + scale_epsilon).astype(jnp.bfloat16)
    new_ms[...] = m_top
    new_vs[...] = v_top
    dither = noise[...].astype(jnp.float32)
    m_value = m_new * (LEVELS / m_top.astype(jnp.float32)) + (dither - 0.5)
    v_value = v_new * (LEVELS / v_top.astype(jnp.float32)) + dither
    new_m[...] = jnp.clip(m_value, -1.0 * LEVELS, 1.0 * LEVELS).astype(jnp.bfloat16)
    new_v[...] = jnp.clip(v_value, 0.0, 1.0 * LEVELS).astype(jnp.bfloat16)


def adam(grads, weight, m_code, v_code, m_scale, v_scale, noise):
    rows, width = weight.shape
    block = min(256, rows)
    wide = pl.BlockSpec((block, width), lambda i: (i, 0))
    thin = pl.BlockSpec((block, 1), lambda i: (i, 0))
    big = jax.ShapeDtypeStruct((rows, width), jnp.bfloat16)
    small = jax.ShapeDtypeStruct((rows, 1), jnp.bfloat16)
    return pl.pallas_call(
        adam_kernel,
        grid=(rows // block,),
        out_shape=(big, big, big, small, small),
        in_specs=[wide, wide, wide, wide, thin, thin, wide],
        out_specs=(wide, wide, wide, thin, thin),
        name="adam",
        cost_estimate=pl.CostEstimate(
            flops=30 * rows * width, bytes_accessed=16 * rows * width, transcendentals=2 * rows * width
        ),
    )(grads, weight, m_code, v_code, m_scale, v_scale, noise)


def on_device(
    tokens,
    routes,
    gates,
    cotangent,
    owner_before,
    owner_after,
    weights,
    m_codes,
    v_codes,
    m_scales,
    v_scales,
    noise,
):
    expert_count = lax.axis_size("expert")
    me = lax.axis_index("expert")
    slot_ids = jnp.arange(expert_count, dtype=jnp.int32)
    matches = (owner_after[None, :] == slot_ids[:, None]).astype(jnp.int32)
    source_slot = jnp.sum(matches * owner_before[None, :], axis=1)
    my_match = (owner_after == me).astype(jnp.int32)
    my_expert = jnp.sum(my_match * slot_ids)
    my_source = jnp.sum(my_match * owner_before)
    rows_dp = weights.shape[2]
    hidden_units = weights.shape[3]
    model_width = tokens.shape[1]
    token_count = tokens.shape[0]
    piece = 2 * rows_dp // expert_count

    def spread(array):
        shaped = array.reshape(expert_count, piece, hidden_units)
        return lax.all_to_all(shaped, "expert", split_axis=0, concat_axis=0, tiled=True)

    def collect(array):
        regrouped = jnp.take(array, source_slot, axis=0)
        return lax.all_to_all(regrouped, "expert", split_axis=0, concat_axis=0, tiled=True)

    dense_gates = jnp.sum(
        jnp.where(routes[:, :, None] == slot_ids[None, None, :], gates[:, :, None], 0.0), axis=1
    ).T
    all_gates = lax.all_gather(dense_gates, "expert", axis=0, tiled=False)
    gate = lax.dynamic_index_in_dim(all_gates, my_expert, axis=1, keepdims=False).reshape(-1)
    all_tokens = lax.all_gather(tokens, "expert", axis=0, tiled=True)
    all_cotangent = lax.all_gather(cotangent, "expert", axis=0, tiled=True)
    scales = jnp.concatenate([m_scales.reshape(1, 2 * rows_dp), v_scales.reshape(1, 2 * rows_dp)])
    all_scales = lax.all_gather(scales, "expert", axis=0, tiled=False)
    old_scales = lax.dynamic_index_in_dim(all_scales, my_source, axis=0, keepdims=False)

    moved_weights = collect(spread(weights)).reshape(2, rows_dp, hidden_units)
    moved_m = collect(spread(m_codes)).reshape(2 * rows_dp, hidden_units)
    moved_v = collect(spread(v_codes)).reshape(2 * rows_dp, hidden_units)

    gated = (gate[:, None] * all_cotangent.astype(jnp.float32)).astype(jnp.bfloat16)
    scale_model = model_width ** (-0.5)
    scale_hidden = hidden_units ** (-0.5)
    full_weights = lax.all_gather(moved_weights, "dp", axis=1, tiled=True)
    pre = jnp.dot(all_tokens, full_weights[0], preferred_element_type=jnp.float32) * scale_model
    back = jnp.dot(gated, full_weights[1], preferred_element_type=jnp.float32) * scale_hidden
    sigmoid_pre = jax.nn.sigmoid(pre)
    hidden = (pre * sigmoid_pre).astype(jnp.bfloat16)
    pre_grad = (back * sigmoid_pre * (1.0 + pre * (1.0 - sigmoid_pre))).astype(jnp.bfloat16)
    up_part = transposed_dot(all_tokens, pre_grad) * scale_model
    down_part = transposed_dot(gated, hidden) * scale_hidden
    summed = lax.psum_scatter(
        jnp.stack([up_part.astype(jnp.bfloat16), down_part.astype(jnp.bfloat16)]),
        "dp",
        scatter_dimension=1,
        tiled=True,
    )
    new_w, new_m, new_v, new_ms, new_vs = adam(
        summed.reshape(2 * rows_dp, hidden_units),
        moved_weights.reshape(2 * rows_dp, hidden_units),
        moved_m,
        moved_v,
        old_scales[0][:, None],
        old_scales[1][:, None],
        noise.reshape(2 * rows_dp, hidden_units),
    )
    return (
        new_w.reshape(2, 1, rows_dp, hidden_units),
        new_m.reshape(2, 1, rows_dp, hidden_units),
        new_v.reshape(2, 1, rows_dp, hidden_units),
        new_ms.reshape(2, 1, rows_dp),
        new_vs.reshape(2, 1, rows_dp),
    )


def solution(mesh):
    placed = (
        P(("expert", "dp"), None),
        P(("expert", "dp"), None),
        P(("expert", "dp"), None),
        P(("expert", "dp"), None),
        P(),
        P(),
        P(None, "expert", "dp", None),
        P(None, "expert", "dp", None),
        P(None, "expert", "dp", None),
        P(None, "expert", "dp"),
        P(None, "expert", "dp"),
        P(None, "expert", "dp", None),
    )
    return jax.shard_map(
        on_device,
        mesh=mesh,
        in_specs=placed,
        out_specs=(
            P(None, "expert", "dp", None),
            P(None, "expert", "dp", None),
            P(None, "expert", "dp", None),
            P(None, "expert", "dp"),
            P(None, "expert", "dp"),
        ),
        check_vma=False,
    )
```

```python
import functools

import jax
import jax.numpy as jnp
from jax import lax
from jax.experimental import pallas as pl
from jax.experimental.pallas import tpu as pltpu
from jax.sharding import PartitionSpec as P

LEVELS = 7


learn_rate = 0.1
beta_one = 0.9
beta_two = 0.95
adam_step = 20.0
adam_epsilon = 1e-08
scale_epsilon = 1e-06


def transposed_dot(left, right):
    return lax.dot_general(
        left, right, (((0,), (0,)), ((), ())), preferred_element_type=jnp.float32
    )


def adam_kernel(parts, *refs):
    weight, m_code, v_code, m_scale, v_scale, noise, new_w, new_m, new_v, new_ms, new_vs = refs[parts:]
    grads = refs[0][...].astype(jnp.float32)
    for part in refs[1:parts]:
        grads += part[...].astype(jnp.float32)
    m_old = m_code[...].astype(jnp.float32) * (m_scale[...].astype(jnp.float32) / LEVELS)
    v_old = v_code[...].astype(jnp.float32) * (v_scale[...].astype(jnp.float32) / LEVELS)
    m_new = beta_one * m_old + (1.0 - beta_one) * grads
    v_new = beta_two * v_old + (1.0 - beta_two) * grads * grads
    direction = (
        m_new
        * (1.0 / (1.0 - beta_one**adam_step))
        / (jnp.sqrt(v_new * (1.0 / (1.0 - beta_two**adam_step))) + adam_epsilon)
    )
    new_w[...] = (weight[...].astype(jnp.float32) - learn_rate * direction).astype(jnp.bfloat16)
    m_top = (jnp.max(jnp.abs(m_new), axis=1, keepdims=True) + scale_epsilon).astype(jnp.bfloat16)
    v_top = (jnp.max(v_new, axis=1, keepdims=True) + scale_epsilon).astype(jnp.bfloat16)
    new_ms[...] = m_top
    new_vs[...] = v_top
    dither = noise[...].astype(jnp.float32)
    m_value = m_new * (LEVELS / m_top.astype(jnp.float32)) + (dither - 0.5)
    v_value = v_new * (LEVELS / v_top.astype(jnp.float32)) + dither
    new_m[...] = jnp.clip(m_value, -1.0 * LEVELS, 1.0 * LEVELS).astype(jnp.bfloat16)
    new_v[...] = jnp.clip(v_value, 0.0, 1.0 * LEVELS).astype(jnp.bfloat16)


def adam(grads, weight, m_code, v_code, m_scale, v_scale, noise):
    rows, width = weight.shape
    block = min(256, rows)
    wide = pl.BlockSpec((block, width), lambda i: (i, 0))
    thin = pl.BlockSpec((block, 1), lambda i: (i, 0))
    big = jax.ShapeDtypeStruct((rows, width), jnp.bfloat16)
    small = jax.ShapeDtypeStruct((rows, 1), jnp.bfloat16)
    return pl.pallas_call(
        functools.partial(adam_kernel, len(grads)),
        grid=(rows // block,),
        out_shape=(big, big, big, small, small),
        in_specs=[wide] * len(grads) + [wide, wide, wide, thin, thin, wide],
        out_specs=(wide, wide, wide, thin, thin),
        name="adam",
        cost_estimate=pl.CostEstimate(
            flops=30 * rows * width, bytes_accessed=16 * rows * width, transcendentals=2 * rows * width
        ),
    )(*grads, weight, m_code, v_code, m_scale, v_scale, noise)


def on_device(
    tokens,
    routes,
    gates,
    cotangent,
    owner_before,
    owner_after,
    weights,
    m_codes,
    v_codes,
    m_scales,
    v_scales,
    noise,
):
    expert_count = lax.axis_size("expert")
    me = lax.axis_index("expert")
    slot_ids = jnp.arange(expert_count, dtype=jnp.int32)
    matches = (owner_after[None, :] == slot_ids[:, None]).astype(jnp.int32)
    source_slot = jnp.sum(matches * owner_before[None, :], axis=1)
    my_match = (owner_after == me).astype(jnp.int32)
    my_expert = jnp.sum(my_match * slot_ids)
    my_source = jnp.sum(my_match * owner_before)
    rows_dp = weights.shape[2]
    hidden_units = weights.shape[3]
    model_width = tokens.shape[1]
    token_count = tokens.shape[0]
    piece = 2 * rows_dp // expert_count

    dp_count = lax.axis_size("dp")
    my_dp = lax.axis_index("dp")

    def spread(array):
        shaped = array.reshape(expert_count, piece, hidden_units)
        return lax.all_to_all(shaped, "expert", split_axis=0, concat_axis=0, tiled=True)

    def collect(array):
        return lax.all_to_all(array, "expert", split_axis=0, concat_axis=0, tiled=True)

    def regroup(array):
        return array.at[source_slot].get(mode="promise_in_bounds")

    def shift(array, step):
        ring = [(i, (i + step) % dp_count) for i in range(dp_count)]
        return lax.ppermute(array, "dp", ring)

    dense_gates = jnp.sum(
        jnp.where(routes[:, :, None] == slot_ids[None, None, :], gates[:, :, None], 0.0), axis=1
    ).T
    scales = jnp.concatenate([m_scales.reshape(-1), v_scales.reshape(-1)]).astype(jnp.float32)
    small = jnp.concatenate([dense_gates, scales.reshape(-1, token_count)])
    all_small = lax.all_gather(small, "expert", axis=0, tiled=False)
    all_tokens = lax.all_gather(tokens, "expert", axis=0, tiled=True)
    all_cotangent = lax.all_gather(cotangent, "expert", axis=0, tiled=True)

    weights, all_small = lax.optimization_barrier((weights, all_small))
    gate = lax.dynamic_index_in_dim(all_small, my_expert, axis=1, keepdims=False).reshape(-1)
    old_scales = lax.dynamic_index_in_dim(all_small, my_source, axis=0, keepdims=False)[expert_count:]
    old_scales = old_scales.reshape(2, 2 * rows_dp)
    moved_weights = collect(regroup(spread(weights)))
    moved_weights, m_codes = lax.optimization_barrier((moved_weights, m_codes))
    m_spread = spread(m_codes)
    m_spread, v_codes = lax.optimization_barrier((m_spread, v_codes))
    v_spread = spread(v_codes)
    m_ready, v_spread = lax.optimization_barrier((regroup(m_spread), v_spread))
    moved_m = collect(m_ready)
    v_ready, moved_m = lax.optimization_barrier((regroup(v_spread), moved_m))
    moved_v = collect(v_ready)

    own_rows = moved_weights.reshape(2, rows_dp, hidden_units)
    full_weights = jnp.zeros((2, dp_count * rows_dp, hidden_units), jnp.bfloat16)
    full_weights = lax.dynamic_update_slice(full_weights, own_rows, (0, my_dp * rows_dp, 0))
    for step in range(1, dp_count):
        start = (my_dp - step) % dp_count * rows_dp
        full_weights = lax.dynamic_update_slice(full_weights, shift(own_rows, step), (0, start, 0))
    gated = (gate[:, None] * all_cotangent.astype(jnp.float32)).astype(jnp.bfloat16)
    scale_model = model_width ** (-0.5)
    scale_hidden = hidden_units ** (-0.5)
    pre = jnp.dot(all_tokens, full_weights[0], preferred_element_type=jnp.float32) * scale_model
    back = jnp.dot(gated, full_weights[1], preferred_element_type=jnp.float32) * scale_hidden
    sigmoid_pre = jax.nn.sigmoid(pre)
    hidden = (pre * sigmoid_pre).astype(jnp.bfloat16)
    pre_grad = (back * sigmoid_pre * (1.0 + pre * (1.0 - sigmoid_pre))).astype(jnp.bfloat16)
    up_part = (transposed_dot(all_tokens, pre_grad) * scale_model).astype(jnp.bfloat16)
    down_part = (transposed_dot(gated, hidden) * scale_hidden).astype(jnp.bfloat16)
    part = jnp.stack([up_part, down_part])
    grads = []
    for step in range(dp_count):
        start = (my_dp + step) % dp_count * rows_dp
        mine = lax.dynamic_slice(part, (0, start, 0), (2, rows_dp, hidden_units))
        grads.append((shift(mine, step) if step else mine).reshape(2 * rows_dp, hidden_units))
    new_w, new_m, new_v, new_ms, new_vs = adam(
        grads,
        moved_weights.reshape(2 * rows_dp, hidden_units),
        moved_m.reshape(2 * rows_dp, hidden_units),
        moved_v.reshape(2 * rows_dp, hidden_units),
        old_scales[0][:, None],
        old_scales[1][:, None],
        noise.reshape(2 * rows_dp, hidden_units),
    )
    return (
        new_w.reshape(2, 1, rows_dp, hidden_units),
        new_m.reshape(2, 1, rows_dp, hidden_units),
        new_v.reshape(2, 1, rows_dp, hidden_units),
        new_ms.reshape(2, 1, rows_dp),
        new_vs.reshape(2, 1, rows_dp),
    )


def solution(mesh):
    placed = (
        P(("expert", "dp"), None),
        P(("expert", "dp"), None),
        P(("expert", "dp"), None),
        P(("expert", "dp"), None),
        P(),
        P(),
        P(None, "expert", "dp", None),
        P(None, "expert", "dp", None),
        P(None, "expert", "dp", None),
        P(None, "expert", "dp"),
        P(None, "expert", "dp"),
        P(None, "expert", "dp", None),
    )
    return jax.shard_map(
        on_device,
        mesh=mesh,
        in_specs=placed,
        out_specs=(
            P(None, "expert", "dp", None),
            P(None, "expert", "dp", None),
            P(None, "expert", "dp", None),
            P(None, "expert", "dp"),
            P(None, "expert", "dp"),
        ),
        check_vma=False,
    )
```

```python
import functools

import jax
import jax.numpy as jnp
from jax import lax
from jax.experimental import pallas as pl
from jax.experimental.pallas import tpu as pltpu
from jax.sharding import PartitionSpec as P

LEVELS = 7


learn_rate = 0.1
beta_one = 0.9
beta_two = 0.95
adam_step = 20.0
adam_epsilon = 1e-08
scale_epsilon = 1e-06


def transposed_dot(left, right):
    return lax.dot_general(
        left, right, (((0,), (0,)), ((), ())), preferred_element_type=jnp.float32
    )


def adam_kernel(parts, *refs):
    weight, m_code, v_code, m_scale, v_scale, noise, new_w, new_m, new_v, new_ms, new_vs = refs[parts:]
    grads = refs[0][...].astype(jnp.float32)
    for part in refs[1:parts]:
        grads += part[...].astype(jnp.float32)
    m_old = m_code[...].astype(jnp.float32) * (m_scale[...].astype(jnp.float32) / LEVELS)
    v_old = v_code[...].astype(jnp.float32) * (v_scale[...].astype(jnp.float32) / LEVELS)
    m_new = beta_one * m_old + (1.0 - beta_one) * grads
    v_new = beta_two * v_old + (1.0 - beta_two) * grads * grads
    direction = (
        m_new
        * (1.0 / (1.0 - beta_one**adam_step))
        / (jnp.sqrt(v_new * (1.0 / (1.0 - beta_two**adam_step))) + adam_epsilon)
    )
    new_w[...] = (weight[...].astype(jnp.float32) - learn_rate * direction).astype(jnp.bfloat16)
    m_top = (jnp.max(jnp.abs(m_new), axis=1, keepdims=True) + scale_epsilon).astype(jnp.bfloat16)
    v_top = (jnp.max(v_new, axis=1, keepdims=True) + scale_epsilon).astype(jnp.bfloat16)
    new_ms[...] = m_top
    new_vs[...] = v_top
    dither = noise[...].astype(jnp.float32)
    m_value = m_new * (LEVELS / m_top.astype(jnp.float32)) + (dither - 0.5)
    v_value = v_new * (LEVELS / v_top.astype(jnp.float32)) + dither
    new_m[...] = jnp.clip(m_value, -1.0 * LEVELS, 1.0 * LEVELS).astype(jnp.bfloat16)
    new_v[...] = jnp.clip(v_value, 0.0, 1.0 * LEVELS).astype(jnp.bfloat16)


def adam(grads, weight, m_code, v_code, m_scale, v_scale, noise):
    rows, width = weight.shape
    block = min(256, rows)
    wide = pl.BlockSpec((block, width), lambda i: (i, 0))
    thin = pl.BlockSpec((block, 1), lambda i: (i, 0))
    big = jax.ShapeDtypeStruct((rows, width), jnp.bfloat16)
    small = jax.ShapeDtypeStruct((rows, 1), jnp.bfloat16)
    return pl.pallas_call(
        functools.partial(adam_kernel, len(grads)),
        grid=(rows // block,),
        out_shape=(big, big, big, small, small),
        in_specs=[wide] * len(grads) + [wide, wide, wide, thin, thin, wide],
        out_specs=(wide, wide, wide, thin, thin),
        name="adam",
        cost_estimate=pl.CostEstimate(
            flops=30 * rows * width, bytes_accessed=16 * rows * width, transcendentals=2 * rows * width
        ),
    )(*grads, weight, m_code, v_code, m_scale, v_scale, noise)


def on_device(
    tokens,
    routes,
    gates,
    cotangent,
    owner_before,
    owner_after,
    weights,
    m_codes,
    v_codes,
    m_scales,
    v_scales,
    noise,
):
    expert_count = lax.axis_size("expert")
    me = lax.axis_index("expert")
    slot_ids = jnp.arange(expert_count, dtype=jnp.int32)
    matches = (owner_after[None, :] == slot_ids[:, None]).astype(jnp.int32)
    source_slot = jnp.sum(matches * owner_before[None, :], axis=1)
    my_match = (owner_after == me).astype(jnp.int32)
    my_expert = jnp.sum(my_match * slot_ids)
    my_source = jnp.sum(my_match * owner_before)
    rows_dp = weights.shape[2]
    hidden_units = weights.shape[3]
    model_width = tokens.shape[1]
    token_count = tokens.shape[0]
    piece = 2 * rows_dp // expert_count

    dp_count = lax.axis_size("dp")
    my_dp = lax.axis_index("dp")

    def spread(array):
        shaped = array.reshape(expert_count, piece, hidden_units)
        return lax.all_to_all(shaped, "expert", split_axis=0, concat_axis=0, tiled=True)

    def collect(array):
        return lax.all_to_all(array, "expert", split_axis=0, concat_axis=0, tiled=True)

    def regroup(array):
        return array.at[source_slot].get(mode="promise_in_bounds")

    def shift(array, step):
        ring = [(i, (i + step) % dp_count) for i in range(dp_count)]
        return lax.ppermute(array, "dp", ring)

    dense_gates = jnp.sum(
        jnp.where(routes[:, :, None] == slot_ids[None, None, :], gates[:, :, None], 0.0), axis=1
    ).T
    scales = jnp.concatenate([m_scales.reshape(-1), v_scales.reshape(-1)]).astype(jnp.float32)
    small = jnp.concatenate([dense_gates, scales.reshape(-1, token_count)])
    all_small = lax.all_gather(small, "expert", axis=0, tiled=False)
    inner = 1
    while inner * inner * 4 <= expert_count and expert_count % (inner * 2) == 0:
        inner *= 2
    outer = expert_count // inner
    lines = [[i + inner * k for k in range(outer)] for i in range(inner)]
    planes = [[inner * k + i for i in range(inner)] for k in range(outer)]

    def gather_rows(array):
        line = lax.all_gather(array, "expert", axis=0, tiled=True, axis_index_groups=lines)
        return lax.all_gather(line, "expert", axis=0, tiled=True, axis_index_groups=planes)

    all_tokens = gather_rows(tokens)
    all_cotangent = gather_rows(cotangent)

    weights_ready, all_small = lax.optimization_barrier((regroup(spread(weights)), all_small))
    gate = lax.dynamic_index_in_dim(all_small, my_expert, axis=1, keepdims=False)
    gate = gate.reshape(outer, inner, token_count).swapaxes(0, 1).reshape(-1)
    old_scales = lax.dynamic_index_in_dim(all_small, my_source, axis=0, keepdims=False)[expert_count:]
    old_scales = old_scales.reshape(2, 2 * rows_dp)
    moved_weights = collect(weights_ready)
    moved_weights, m_codes = lax.optimization_barrier((moved_weights, m_codes))
    m_spread = spread(m_codes)
    m_spread, v_codes = lax.optimization_barrier((m_spread, v_codes))
    v_spread = spread(v_codes)
    m_ready, v_spread = lax.optimization_barrier((regroup(m_spread), v_spread))
    moved_m = collect(m_ready)
    v_ready, moved_m = lax.optimization_barrier((regroup(v_spread), moved_m))
    moved_v = collect(v_ready)

    own_rows = moved_weights.reshape(2, rows_dp, hidden_units)
    full_weights = jnp.zeros((2, dp_count * rows_dp, hidden_units), jnp.bfloat16)
    full_weights = lax.dynamic_update_slice(full_weights, own_rows, (0, my_dp * rows_dp, 0))
    for step in range(1, dp_count):
        start = (my_dp - step) % dp_count * rows_dp
        full_weights = lax.dynamic_update_slice(full_weights, shift(own_rows, step), (0, start, 0))
    gated = (gate[:, None] * all_cotangent.astype(jnp.float32)).astype(jnp.bfloat16)
    scale_model = model_width ** (-0.5)
    scale_hidden = hidden_units ** (-0.5)
    pre = jnp.dot(all_tokens, full_weights[0], preferred_element_type=jnp.float32) * scale_model
    back = jnp.dot(gated, full_weights[1], preferred_element_type=jnp.float32) * scale_hidden
    sigmoid_pre = jax.nn.sigmoid(pre)
    hidden = (pre * sigmoid_pre).astype(jnp.bfloat16)
    pre_grad = (back * sigmoid_pre * (1.0 + pre * (1.0 - sigmoid_pre))).astype(jnp.bfloat16)
    up_part = (transposed_dot(all_tokens, pre_grad) * scale_model).astype(jnp.bfloat16)
    down_part = (transposed_dot(gated, hidden) * scale_hidden).astype(jnp.bfloat16)
    part = jnp.stack([up_part, down_part])
    grads = []
    for step in range(dp_count):
        start = (my_dp + step) % dp_count * rows_dp
        mine = lax.dynamic_slice(part, (0, start, 0), (2, rows_dp, hidden_units))
        grads.append((shift(mine, step) if step else mine).reshape(2 * rows_dp, hidden_units))
    new_w, new_m, new_v, new_ms, new_vs = adam(
        grads,
        moved_weights.reshape(2 * rows_dp, hidden_units),
        moved_m.reshape(2 * rows_dp, hidden_units),
        moved_v.reshape(2 * rows_dp, hidden_units),
        old_scales[0][:, None],
        old_scales[1][:, None],
        noise.reshape(2 * rows_dp, hidden_units),
    )
    return (
        new_w.reshape(2, 1, rows_dp, hidden_units),
        new_m.reshape(2, 1, rows_dp, hidden_units),
        new_v.reshape(2, 1, rows_dp, hidden_units),
        new_ms.reshape(2, 1, rows_dp),
        new_vs.reshape(2, 1, rows_dp),
    )


def solution(mesh):
    placed = (
        P(("expert", "dp"), None),
        P(("expert", "dp"), None),
        P(("expert", "dp"), None),
        P(("expert", "dp"), None),
        P(),
        P(),
        P(None, "expert", "dp", None),
        P(None, "expert", "dp", None),
        P(None, "expert", "dp", None),
        P(None, "expert", "dp"),
        P(None, "expert", "dp"),
        P(None, "expert", "dp", None),
    )
    return jax.shard_map(
        on_device,
        mesh=mesh,
        in_specs=placed,
        out_specs=(
            P(None, "expert", "dp", None),
            P(None, "expert", "dp", None),
            P(None, "expert", "dp", None),
            P(None, "expert", "dp"),
            P(None, "expert", "dp"),
        ),
        check_vma=False,
    )
```

```python
import functools

import jax
import jax.numpy as jnp
from jax import lax
from jax.experimental import pallas as pl
from jax.experimental.pallas import tpu as pltpu
from jax.sharding import PartitionSpec as P

LEVELS = 7


learn_rate = 0.1
beta_one = 0.9
beta_two = 0.95
adam_step = 20.0
adam_epsilon = 1e-08
scale_epsilon = 1e-06


def transposed_dot(left, right):
    return lax.dot_general(
        left, right, (((0,), (0,)), ((), ())), preferred_element_type=jnp.float32
    )


def adam_kernel(parts, *refs):
    weight, m_code, v_code, m_scale, v_scale, noise, new_w, new_m, new_v, new_ms, new_vs = refs[parts:]
    grads = refs[0][...].astype(jnp.float32)
    for part in refs[1:parts]:
        grads += part[...].astype(jnp.float32)
    m_old = m_code[...].astype(jnp.float32) * (m_scale[...].astype(jnp.float32) / LEVELS)
    v_old = v_code[...].astype(jnp.float32) * (v_scale[...].astype(jnp.float32) / LEVELS)
    m_new = beta_one * m_old + (1.0 - beta_one) * grads
    v_new = beta_two * v_old + (1.0 - beta_two) * grads * grads
    direction = (
        m_new
        * (1.0 / (1.0 - beta_one**adam_step))
        / (jnp.sqrt(v_new * (1.0 / (1.0 - beta_two**adam_step))) + adam_epsilon)
    )
    new_w[...] = (weight[...].astype(jnp.float32) - learn_rate * direction).astype(jnp.bfloat16)
    m_top = (jnp.max(jnp.abs(m_new), axis=1, keepdims=True) + scale_epsilon).astype(jnp.bfloat16)
    v_top = (jnp.max(v_new, axis=1, keepdims=True) + scale_epsilon).astype(jnp.bfloat16)
    new_ms[...] = m_top
    new_vs[...] = v_top
    dither = noise[...].astype(jnp.float32)
    m_value = m_new * (LEVELS / m_top.astype(jnp.float32)) + (dither - 0.5)
    v_value = v_new * (LEVELS / v_top.astype(jnp.float32)) + dither
    new_m[...] = jnp.clip(m_value, -1.0 * LEVELS, 1.0 * LEVELS).astype(jnp.bfloat16)
    new_v[...] = jnp.clip(v_value, 0.0, 1.0 * LEVELS).astype(jnp.bfloat16)


def adam(grads, weight, m_code, v_code, m_scale, v_scale, noise):
    rows, width = weight.shape
    block = min(256, rows)
    wide = pl.BlockSpec((block, width), lambda i: (i, 0))
    thin = pl.BlockSpec((block, 1), lambda i: (i, 0))
    big = jax.ShapeDtypeStruct((rows, width), jnp.bfloat16)
    small = jax.ShapeDtypeStruct((rows, 1), jnp.bfloat16)
    return pl.pallas_call(
        functools.partial(adam_kernel, len(grads)),
        grid=(rows // block,),
        out_shape=(big, big, big, small, small),
        in_specs=[wide] * len(grads) + [wide, wide, wide, thin, thin, wide],
        out_specs=(wide, wide, wide, thin, thin),
        name="adam",
        cost_estimate=pl.CostEstimate(
            flops=30 * rows * width, bytes_accessed=16 * rows * width, transcendentals=2 * rows * width
        ),
    )(*grads, weight, m_code, v_code, m_scale, v_scale, noise)


def on_device(
    tokens,
    routes,
    gates,
    cotangent,
    owner_before,
    owner_after,
    weights,
    m_codes,
    v_codes,
    m_scales,
    v_scales,
    noise,
):
    expert_count = lax.axis_size("expert")
    me = lax.axis_index("expert")
    slot_ids = jnp.arange(expert_count, dtype=jnp.int32)
    matches = (owner_after[None, :] == slot_ids[:, None]).astype(jnp.int32)
    source_slot = jnp.sum(matches * owner_before[None, :], axis=1)
    my_match = (owner_after == me).astype(jnp.int32)
    my_expert = jnp.sum(my_match * slot_ids)
    my_source = jnp.sum(my_match * owner_before)
    rows_dp = weights.shape[2]
    hidden_units = weights.shape[3]
    model_width = tokens.shape[1]
    token_count = tokens.shape[0]
    piece = 2 * rows_dp // expert_count

    dp_count = lax.axis_size("dp")
    my_dp = lax.axis_index("dp")

    def spread(array):
        shaped = array.reshape(expert_count, piece, hidden_units)
        return lax.all_to_all(shaped, "expert", split_axis=0, concat_axis=0, tiled=True)

    def collect(array):
        return lax.all_to_all(array, "expert", split_axis=0, concat_axis=0, tiled=True)

    def regroup(array):
        return array.at[source_slot].get(mode="promise_in_bounds")

    def shift(array, step):
        ring = [(i, (i + step) % dp_count) for i in range(dp_count)]
        return lax.ppermute(array, "dp", ring)

    dense_gates = jnp.sum(
        jnp.where(routes[:, :, None] == slot_ids[None, None, :], gates[:, :, None], 0.0), axis=1
    ).T
    scales = jnp.concatenate([m_scales.reshape(-1), v_scales.reshape(-1)]).astype(jnp.float32)
    small = jnp.concatenate([dense_gates, scales.reshape(-1, token_count)])
    all_small = lax.all_gather(small, "expert", axis=0, tiled=False)
    inner = 1
    while inner * inner * 4 <= expert_count and expert_count % (inner * 2) == 0:
        inner *= 2
    outer = expert_count // inner
    lines = [[i + inner * k for k in range(outer)] for i in range(inner)]
    planes = [[inner * k + i for i in range(inner)] for k in range(outer)]

    def gather_line(array):
        return lax.all_gather(array, "expert", axis=0, tiled=True, axis_index_groups=lines)

    def gather_plane(array):
        return lax.all_gather(array, "expert", axis=0, tiled=True, axis_index_groups=planes)

    line_tokens, all_small = lax.optimization_barrier((gather_line(tokens), all_small))
    all_tokens = gather_plane(line_tokens)
    all_cotangent = gather_plane(gather_line(cotangent))

    weights_ready, all_small = lax.optimization_barrier((regroup(spread(weights)), all_small))
    gate = lax.dynamic_index_in_dim(all_small, my_expert, axis=1, keepdims=False)
    gate = gate.reshape(outer, inner, token_count).swapaxes(0, 1).reshape(-1)
    old_scales = lax.dynamic_index_in_dim(all_small, my_source, axis=0, keepdims=False)[expert_count:]
    old_scales = old_scales.reshape(2, 2 * rows_dp)
    moved_weights = collect(weights_ready)
    moved_weights, m_codes = lax.optimization_barrier((moved_weights, m_codes))
    m_spread = spread(m_codes)
    m_spread, v_codes = lax.optimization_barrier((m_spread, v_codes))
    v_spread = spread(v_codes)
    m_ready, v_spread = lax.optimization_barrier((regroup(m_spread), v_spread))
    moved_m = collect(m_ready)
    v_ready, moved_m = lax.optimization_barrier((regroup(v_spread), moved_m))
    moved_v = collect(v_ready)
    moved_m, all_cotangent = lax.optimization_barrier((moved_m, all_cotangent))

    own_rows = moved_weights.reshape(2, rows_dp, hidden_units)
    full_weights = jnp.zeros((2, dp_count * rows_dp, hidden_units), jnp.bfloat16)
    full_weights = lax.dynamic_update_slice(full_weights, own_rows, (0, my_dp * rows_dp, 0))
    for step in range(1, dp_count):
        start = (my_dp - step) % dp_count * rows_dp
        full_weights = lax.dynamic_update_slice(full_weights, shift(own_rows, step), (0, start, 0))
    gated = (gate[:, None] * all_cotangent.astype(jnp.float32)).astype(jnp.bfloat16)
    scale_model = model_width ** (-0.5)
    scale_hidden = hidden_units ** (-0.5)
    pre = jnp.dot(all_tokens, full_weights[0], preferred_element_type=jnp.float32) * scale_model
    back = jnp.dot(gated, full_weights[1], preferred_element_type=jnp.float32) * scale_hidden
    sigmoid_pre = jax.nn.sigmoid(pre)
    hidden = (pre * sigmoid_pre).astype(jnp.bfloat16)
    pre_grad = (back * sigmoid_pre * (1.0 + pre * (1.0 - sigmoid_pre))).astype(jnp.bfloat16)
    up_part = (transposed_dot(all_tokens, pre_grad) * scale_model).astype(jnp.bfloat16)
    down_part = (transposed_dot(gated, hidden) * scale_hidden).astype(jnp.bfloat16)
    part = jnp.stack([up_part, down_part])
    grads = []
    for step in range(dp_count):
        start = (my_dp + step) % dp_count * rows_dp
        mine = lax.dynamic_slice(part, (0, start, 0), (2, rows_dp, hidden_units))
        grads.append((shift(mine, step) if step else mine).reshape(2 * rows_dp, hidden_units))
    new_w, new_m, new_v, new_ms, new_vs = adam(
        grads,
        moved_weights.reshape(2 * rows_dp, hidden_units),
        moved_m.reshape(2 * rows_dp, hidden_units),
        moved_v.reshape(2 * rows_dp, hidden_units),
        old_scales[0][:, None],
        old_scales[1][:, None],
        noise.reshape(2 * rows_dp, hidden_units),
    )
    return (
        new_w.reshape(2, 1, rows_dp, hidden_units),
        new_m.reshape(2, 1, rows_dp, hidden_units),
        new_v.reshape(2, 1, rows_dp, hidden_units),
        new_ms.reshape(2, 1, rows_dp),
        new_vs.reshape(2, 1, rows_dp),
    )


def solution(mesh):
    placed = (
        P(("expert", "dp"), None),
        P(("expert", "dp"), None),
        P(("expert", "dp"), None),
        P(("expert", "dp"), None),
        P(),
        P(),
        P(None, "expert", "dp", None),
        P(None, "expert", "dp", None),
        P(None, "expert", "dp", None),
        P(None, "expert", "dp"),
        P(None, "expert", "dp"),
        P(None, "expert", "dp", None),
    )
    return jax.shard_map(
        on_device,
        mesh=mesh,
        in_specs=placed,
        out_specs=(
            P(None, "expert", "dp", None),
            P(None, "expert", "dp", None),
            P(None, "expert", "dp", None),
            P(None, "expert", "dp"),
            P(None, "expert", "dp"),
        ),
        check_vma=False,
    )
```
